256 devices in a mesh: grid: 8 (over z), snap: 32 (over x, y, core).
Axes of the slice: x: 4, y: 4, z: 8, core: 2. Of those that a mesh axis runs over, the one named last changes fastest.
Arguments:
- snapshots: bfloat16 [16384, 65536], P('grid', 'snap'), may hold values from -6 to 6
- test_matrix: bfloat16 [128, 16384], P(None, 'grid'), may hold values from -0.046875 to 0.046875
- leaf_pivots: int32 [32, 128], P('snap'), may hold values from 0 to 2047, as said below
- leaf_inverse: float32 [32, 128, 128], P('snap'), as said below
- merge_pivots: int32 [31, 128], replicated, may hold values from 0 to 255, as said below
- merge_inverse: float32 [31, 128, 128], replicated, as said below
- skeleton_ids: int32 [128], replicated, may hold values from 0 to 65535, as said below
Outputs:
- skeleton: bfloat16 [16384, 128], P('grid')
- coefficients: bfloat16 [128, 65536], P(None, 'snap')
The draws below stay inside these ranges and needn't reach their ends.
Inputs may be any that keep to these rules, and one draw needn't show every extreme that they name: `leaf_pivots`: each row holds 128 distinct column numbers. `merge_pivots`: each row holds 128 distinct numbers. `skeleton_ids`: the ids that the tree keeps at node 1: leaf b starts with b * 2048 + leaf_pivots[b], each node keeps positions merge_pivots[n - 1] of its children's lists side by side. `leaf_inverse`: upper triangular with a positive diagonal. `merge_inverse`: upper triangular with a positive diagonal.
All inputs are finite; a program needn't handle non-finite values.
Results may differ from the reference program's by a relative error of at most 0.001.
Values may be sent and summed in bfloat16 or wider, within the bound.
No kernel may reach another device: no remote copies, remote signals or barrier semaphores. Data moves between devices by JAX's collectives and lax.ppermute only.
A program may use at most 64 MiB of HBM per device.

```python
import jax
import jax.numpy as jnp
import numpy as np
from jax import lax

RANK = 128
COLS_DEV = 2048
ROWS = 16384
COLS = 65536
BLOCKS = 32


def place_value(listing, target, slot):
    where_now = jnp.argmax(listing == target).astype(jnp.int32)
    moved = listing[slot]
    listing = listing.at[where_now].set(moved)
    return listing.at[slot].set(target)


def leaf_row(sub, block):
    first_key, second_key = jax.random.split(sub)
    listing = jax.random.permutation(first_key, COLS_DEV).astype(jnp.int32)
    target = jnp.where(block == 0, jnp.int32(0), jnp.where(block == BLOCKS - 1, jnp.int32(COLS_DEV - 1), listing[0]))
    listing = place_value(listing, target, 0)
    return jax.random.permutation(second_key, listing[:RANK]).astype(jnp.int32)


def merge_row(sub):
    first_key, second_key = jax.random.split(sub)
    listing = jax.random.permutation(first_key, 2 * RANK).astype(jnp.int32)
    listing = place_value(listing, jnp.int32(0), 0)
    listing = place_value(listing, jnp.int32(RANK), 1)
    listing = place_value(listing, jnp.int32(2 * RANK - 1), 2)
    return jax.random.permutation(second_key, listing[:RANK]).astype(jnp.int32)


def tree_lists(key):
    leaf_key = jax.random.fold_in(key, 11)
    merge_key = jax.random.fold_in(key, 23)
    leaf_lists = jax.vmap(leaf_row)(jax.random.split(leaf_key, BLOCKS), jnp.arange(BLOCKS, dtype=jnp.int32))
    merge_lists = jax.vmap(merge_row)(jax.random.split(merge_key, BLOCKS - 1))
    global_ids = jnp.arange(BLOCKS, dtype=jnp.int32)[:, None] * COLS_DEV + leaf_lists
    node_count = BLOCKS
    while node_count > 1:
        half_count = node_count // 2
        stacked = jnp.concatenate([global_ids[0::2], global_ids[1::2]], axis=1)
        global_ids = jnp.take_along_axis(stacked, merge_lists[half_count - 1:2 * half_count - 1], axis=1)
        node_count = half_count
    return (leaf_lists.astype(jnp.int32), merge_lists.astype(jnp.int32), global_ids[0].astype(jnp.int32))


def triangular(key, count):
    first_key, second_key = jax.random.split(key)
    scales = jnp.exp(jax.random.uniform(first_key, (count, RANK, 1), jnp.float32, jnp.log(0.3), jnp.log(1.0)))
    noise = jax.random.normal(second_key, (count, RANK, RANK), jnp.float32)
    upper = jnp.triu(noise, 1) * (0.4 / jnp.sqrt(jnp.float32(RANK)))
    return scales * (jnp.eye(RANK, dtype=jnp.float32)[None] + upper) / RANK


def draw_leaf_pivots(key, part):
    return tree_lists(key)[0]


def draw_merge_pivots(key, part):
    return tree_lists(key)[1]


def draw_skeleton_ids(key, part):
    return tree_lists(key)[2]


def draw_leaf_inverse(key, part):
    return triangular(jax.random.fold_in(key, 37), BLOCKS)


def draw_merge_inverse(key, part):
    return triangular(jax.random.fold_in(key, 41), BLOCKS - 1)


def shard_levels(rng, shape, shards, least, top_value):
    def one(position, parts):
        draws = jax.random.uniform(jax.random.fold_in(jax.random.fold_in(rng, 6), position), (parts,), jnp.float32, least / len(shards), top_value / len(shards))
        return jnp.repeat(jnp.exp(draws), shape[position] // parts).reshape((-1,) + (1,) * (len(shape) - position - 1))

    level = one(*shards[0])
    for cut in shards[1:]:
        level = level * one(*cut)
    return level


def scatter_about(stream_key, shape, spread, bound, pieces=(), kind=jnp.bfloat16):
    drawn = spread * jax.random.normal(stream_key, shape, jnp.float32)
    if pieces:
        drawn = drawn * shard_levels(stream_key, shape, pieces, -0.22, 0.18)
    return jnp.clip(drawn, -bound, bound).astype(kind)


def setup_inputs(seed: int = 0) -> dict:
    arg_keys = jax.random.split(jax.random.key(seed), 8)
    snapshots = scatter_about(arg_keys[0], (ROWS, COLS), 1.0, 6.0, ((0, 8), (1, 32)))
    test_matrix = scatter_about(arg_keys[1], (RANK, ROWS), ROWS ** -0.5, 0.046875, ((1, 8),))
    leaf_pivots = draw_leaf_pivots(jax.random.fold_in(arg_keys[7], 71), 0)
    leaf_inverse = draw_leaf_inverse(jax.random.fold_in(arg_keys[7], 71), 0)
    merge_pivots = draw_merge_pivots(jax.random.fold_in(arg_keys[7], 71), 0)
    merge_inverse = draw_merge_inverse(jax.random.fold_in(arg_keys[7], 71), 0)
    skeleton_ids = draw_skeleton_ids(jax.random.fold_in(arg_keys[7], 71), 0)
    return {"snapshots": snapshots, "test_matrix": test_matrix, "leaf_pivots": leaf_pivots, "leaf_inverse": leaf_inverse, "merge_pivots": merge_pivots, "merge_inverse": merge_inverse, "skeleton_ids": skeleton_ids}


PRECISE = lax.Precision.HIGHEST


def identify(stacked, pivots, inverse):
    picker = (jnp.arange(stacked.shape[1], dtype=jnp.int32)[:, None] == pivots[None, :]).astype(jnp.float32)
    kept_cols = jnp.dot(stacked, picker, precision=PRECISE)
    projected = jnp.dot(kept_cols.T, stacked, precision=PRECISE)
    coeffs = jnp.dot(inverse, projected, precision=PRECISE)
    chosen_mask = jnp.sum(picker, axis=1)
    coeffs = coeffs * (1.0 - chosen_mask)[None, :] + picker.T
    return kept_cols, coeffs


def reference(snapshots, test_matrix, leaf_pivots, leaf_inverse, merge_pivots, merge_inverse, skeleton_ids):
    def leaf_block(block):
        start = (block * COLS_DEV).astype(jnp.int32)
        columns = lax.dynamic_slice_in_dim(snapshots, start, COLS_DEV, 1)
        sketch = jnp.dot(test_matrix, columns, preferred_element_type=jnp.float32)
        return identify(sketch, leaf_pivots[block], leaf_inverse[block])

    candidates, leaf_coeffs = lax.map(leaf_block, jnp.arange(BLOCKS, dtype=jnp.int32))
    composed = jnp.broadcast_to(jnp.eye(RANK, dtype=jnp.float32), (BLOCKS, RANK, RANK))
    node_count = BLOCKS
    tree_level = 1
    block_ids = np.arange(BLOCKS)
    while node_count > 1:
        half_count = node_count // 2
        stacked = jnp.concatenate([candidates[0::2], candidates[1::2]], axis=2)
        candidates, node_coeffs = jax.vmap(identify)(
            stacked, merge_pivots[half_count - 1:2 * half_count - 1], merge_inverse[half_count - 1:2 * half_count - 1])
        node_index = block_ids >> tree_level
        side_index = (block_ids >> (tree_level - 1)) & 1
        split_coeffs = node_coeffs.reshape(half_count, RANK, 2, RANK)
        portion = split_coeffs[node_index, :, side_index, :]
        composed = jnp.einsum("bij,bjk->bik", portion, composed, precision=PRECISE)
        node_count = half_count
        tree_level = tree_level + 1
    blocks_out = jnp.einsum("bij,bjc->bic", composed, leaf_coeffs, precision=PRECISE).astype(jnp.bfloat16)
    coefficients = jnp.transpose(blocks_out, (1, 0, 2)).reshape(RANK, BLOCKS * COLS_DEV)
    skeleton = jnp.take(snapshots, skeleton_ids, axis=1)
    return skeleton, coefficients
```

```python
import jax
import jax.numpy as jnp
from jax import lax
from jax.experimental import pallas as pl
from jax.experimental.pallas import tpu as pltpu
from jax.sharding import PartitionSpec as P

PRECISE = lax.Precision.HIGHEST
F32 = jnp.float32
BF16 = jnp.bfloat16


GRID = 8
SIDE = 4
CORES = 2
RANK = 128
ROW_BLOCK = 256


def grid_shift(step):
    return [(i, (i + step) % GRID) for i in range(GRID)]


def core_swap():
    return [(i, i ^ 1) for i in range(SIDE * SIDE * CORES)]


def y_shift(step):
    return [
        (x * 8 + y * 2 + c, x * 8 + (y + step) % SIDE * 2 + c)
        for x in range(SIDE)
        for y in range(SIDE)
        for c in range(CORES)
    ]


def x_shift(step):
    return [
        (x * 8 + y * 2 + c, (x + step) % SIDE * 8 + y * 2 + c)
        for x in range(SIDE)
        for y in range(SIDE)
        for c in range(CORES)
    ]


def place():
    snap = lax.axis_index("snap")
    return snap // 8, snap // 2 % SIDE, snap % CORES


def dot(a, b):
    return jnp.dot(a, b, precision=PRECISE, preferred_element_type=F32)


def split(value):
    high = value.astype(BF16)
    low = (value - high.astype(F32)).astype(BF16)
    return high, low


def joined(pair):
    return pair[:RANK].astype(F32) + pair[RANK:].astype(F32)


def pickers(pivots):
    rows = lax.broadcasted_iota(jnp.int32, (RANK, RANK), 0)
    return rows == pivots, rows + RANK == pivots


def select(lower, upper, pivots):
    low_pick, high_pick = pickers(pivots)
    kept = jnp.dot(lower, low_pick.astype(BF16), preferred_element_type=F32) + jnp.dot(
        upper, high_pick.astype(BF16), preferred_element_type=F32
    )
    return kept.astype(BF16)


def portion(kept, own, pivots, side, inverse):
    rows = lax.broadcasted_iota(jnp.int32, (RANK, RANK), 0)
    chosen = (rows + side * RANK == pivots).astype(F32).T
    coeffs = dot(inverse, dot(joined(kept).T, joined(own)))
    mask = jnp.sum(chosen, axis=0, keepdims=True)
    return coeffs * (1.0 - mask) + chosen


def pass_kernel(
    snap_ref, test_ref, piv_ref, ids_ref, cand_ref, minus_ref, plus_ref, hm_ref, hp_ref, own_ref,
    keep_ref, send_ref, buf, acc, hot, sems,
):
    rows, cols = snap_ref.shape
    blocks = rows // ROW_BLOCK
    me = lax.axis_index("grid")
    snap = lax.axis_index("snap")
    core = snap % CORES
    copies = []
    for i in range(blocks):
        span = pl.ds(i * ROW_BLOCK, ROW_BLOCK)
        copy = pltpu.make_async_copy(snap_ref.at[span, :], buf.at[span, :], sems.at[i])
        copy.start()
        copies.append(copy)
    column = lax.broadcasted_iota(jnp.int32, (cols, RANK), 0)
    hot[:, :RANK] = (column == ids_ref[...] - snap * cols).astype(F32).astype(BF16)
    hot[:, RANK:] = (column == piv_ref[...]).astype(F32).astype(BF16)
    cand = jnp.zeros((RANK, RANK), F32)
    for i in range(blocks):
        span = pl.ds(i * ROW_BLOCK, ROW_BLOCK)
        copies[i].wait()
        tile = buf[span, :]
        weights = test_ref[:, span]
        update = jnp.dot(weights, tile, preferred_element_type=F32)
        if i:
            acc[...] += update
        else:
            acc[...] = update
        picked = jnp.dot(tile, hot[...], preferred_element_type=F32).astype(BF16)
        cand = cand + jnp.dot(weights, picked[:, RANK:], preferred_element_type=F32)
        half, inner = divmod(i * ROW_BLOCK, rows // CORES)

        @pl.when(core == half)
        def _():
            keep_ref[pl.ds(inner, ROW_BLOCK), :] = picked[:, :RANK]

        @pl.when(core != half)
        def _():
            send_ref[pl.ds(inner, ROW_BLOCK), :] = picked[:, :RANK]

    cand_ref[...] = cand
    width = cols // GRID

    def chunk(step):
        return acc[:, pl.ds(pl.multiple_of((me + GRID + step) % GRID * width, width), width)]

    minus_ref[:, :width] = chunk(-3)
    minus_ref[:, width:] = chunk(-1)
    plus_ref[:, :width] = chunk(3)
    plus_ref[:, width:] = chunk(1)
    far = chunk(4)
    hm_ref[...] = far[: RANK // 2]
    hp_ref[...] = far[RANK // 2 :]
    own_ref[0] = chunk(0)
    own_ref[1] = chunk(-2)
    own_ref[2] = chunk(2)


def shape(dims, dtype):
    return jax.ShapeDtypeStruct(dims, dtype)


def call(kernel, outs, name, **options):
    return pl.pallas_call(kernel, out_shape=outs, name=name, **options)


def cand_sum_kernel(*refs):
    out_ref = refs[-1]
    total = refs[0][...]
    for ref in refs[1:-1]:
        total = total + ref[...]
    high, low = split(total)
    out_ref[:RANK] = high
    out_ref[RANK:] = low


def level0_kernel(own_ref, other_ref, mp_ref, keep_ref, got_ref, cand_ref, mine_ref, *msg_refs):
    x, y, core = place()
    pivots = mp_ref[pl.ds(15 + x * SIDE + y, 1), :]
    own, other = own_ref[...], other_ref[...]
    first = core == 0
    lower = jnp.where(first, own, other)
    upper = jnp.where(first, other, own)
    cand = select(lower, upper, pivots)
    cand_ref[...] = cand
    for d, msg_ref in enumerate(msg_refs, 1):
        span = pl.ds(pl.multiple_of((y + d) % SIDE * 2 * RANK, 2 * RANK), 2 * RANK)
        msg_ref[: 2 * RANK] = cand
        msg_ref[2 * RANK :] = keep_ref[span, :] + got_ref[span, :]
    span = pl.ds(pl.multiple_of(y * 2 * RANK, 2 * RANK), 2 * RANK)
    mine_ref[...] = keep_ref[span, :] + got_ref[span, :]


def path0_kernel(own_ref, cand_ref, mp_ref, li_ref, mi_ref, out_ref):
    x, y, core = place()
    pivots = mp_ref[pl.ds(15 + x * SIDE + y, 1), :]
    leaf = dot(li_ref[...], joined(own_ref[...]).T)
    part = portion(cand_ref[...], own_ref[...], pivots, core, mi_ref[...])
    out_ref[:, :RANK] = dot(part, leaf)
    out_ref[:, RANK:] = part


def two_levels(stack, at, mp_ref, low_row, high_row):
    first = select(stack[0], stack[1], mp_ref[pl.ds(low_row, 1), :])
    second = select(stack[2], stack[3], mp_ref[pl.ds(low_row + 1, 1), :])
    top = select(first, second, mp_ref[pl.ds(high_row, 1), :])
    return first, second, top


def gather_four(own, msg_refs, at, stack):
    stack[at] = own
    for d, ref in enumerate(msg_refs, 1):
        stack[(at + SIDE - d) % SIDE] = ref[: 2 * RANK]


def level12_kernel(own_ref, mine_ref, r1, r2, r3, mp_ref, cand_ref, msg_ref, stack):
    x, y, core = place()
    gather_four(own_ref[...], (r1, r2, r3), y, stack)
    first, second, top = two_levels(stack, y, mp_ref, 7 + x * 2, 3 + x)
    cand_ref[...] = jnp.where(y < 2, first, second)
    msg_ref[: 2 * RANK] = top
    msg_ref[2 * RANK :] = (
        mine_ref[...] + r1[2 * RANK :] + (r2[2 * RANK :] + r3[2 * RANK :])
    )


def path12_kernel(own_ref, cand_ref, msg_ref, mp_ref, mi_a_ref, mi_b_ref, path_ref, out_ref):
    x, y, core = place()
    low = portion(
        cand_ref[...], own_ref[...], mp_ref[pl.ds(7 + x * 2 + y // 2, 1), :], y % 2, mi_a_ref[...]
    )
    high = portion(
        msg_ref[: 2 * RANK], cand_ref[...], mp_ref[pl.ds(3 + x, 1), :], y // 2, mi_b_ref[...]
    )
    out_ref[...] = dot(high, dot(low, path_ref[...]))


def level34_kernel(
    msg_ref, r1, r2, r3, mp_ref, mi_a_ref, mi_b_ref, path_ref, out_ref, skel_ref, stack
):
    x, y, core = place()
    own = msg_ref[: 2 * RANK]
    skel_ref[...] = msg_ref[2 * RANK :] + r1[2 * RANK :] + (r2[2 * RANK :] + r3[2 * RANK :])
    gather_four(own, (r1, r2, r3), x, stack)
    first, second, top = two_levels(stack, x, mp_ref, 1, 0)
    mid = jnp.where(x < 2, first, second)
    low = portion(mid, own, mp_ref[pl.ds(1 + x // 2, 1), :], x % 2, mi_a_ref[...])
    high = portion(top, mid, mp_ref[pl.ds(0, 1), :], x // 2, mi_b_ref[...])
    out_ref[...] = dot(high, dot(low, path_ref[...]))


def relay_kernel(own_ref, rm_ref, rp_ref, hm_ref, hp_ref, down_ref, up_ref):
    half = RANK // 2
    width = own_ref.shape[2]
    down = own_ref[1] + rm_ref[:, :width]
    up = own_ref[2] + rp_ref[:, :width]
    down_ref[:half] = down[:half] + hm_ref[...]
    down_ref[half:] = down[half:]
    up_ref[:half] = up[:half]
    up_ref[half:] = up[half:] + hp_ref[...]


def final_kernel(path_ref, own_ref, rm_ref, rp_ref, d_ref, u_ref, piv_ref, out_ref):
    width = own_ref.shape[2]
    me = lax.axis_index("grid")
    z = own_ref[0] + rm_ref[:, width:] + rp_ref[:, width:] + (d_ref[...] + u_ref[...])
    rows = lax.broadcasted_iota(jnp.int32, (width, RANK), 0) + me * width
    chosen = (rows == piv_ref[...]).astype(F32).T
    mask = jnp.sum(chosen, axis=0, keepdims=True)
    stacked = jnp.concatenate([z * (1.0 - mask), chosen], axis=0)
    out_ref[...] = dot(path_ref[...], stacked).astype(BF16)


def place_grid_kernel(own_ref, *refs):
    out_ref = refs[-1]
    width = own_ref.shape[1]
    me = lax.axis_index("grid")
    out_ref[:, pl.ds(pl.multiple_of(me * width, width), width)] = own_ref[...]
    for d, ref in enumerate(refs[:-1], 1):
        at = (me + GRID - d) % GRID
        out_ref[:, pl.ds(pl.multiple_of(at * width, width), width)] = ref[...]


def place_y_kernel(own_ref, r1, r2, r3, out_ref):
    x, y, core = place()
    height = own_ref.shape[0]
    out_ref[pl.ds(pl.multiple_of(y * height, height), height), :] = own_ref[...]
    for d, ref in enumerate((r1, r2, r3), 1):
        at = (y + SIDE - d) % SIDE
        out_ref[pl.ds(pl.multiple_of(at * height, height), height), :] = ref[...]


def place_core_kernel(own_ref, other_ref, out_ref):
    x, y, core = place()
    height = own_ref.shape[0]
    out_ref[pl.ds(pl.multiple_of(core * height, height), height), :] = own_ref[...]
    out_ref[pl.ds(pl.multiple_of((1 - core) * height, height), height), :] = other_ref[...]


def per_device(
    snapshots, test_matrix, leaf_pivots, leaf_inverse, merge_pivots, merge_inverse, skeleton_ids
):
    rows, cols = snapshots.shape
    width = cols // GRID
    half = rows // CORES
    x, y, core = place()
    vmem = pl.BlockSpec(memory_space=pltpu.VMEM)
    whole = pl.BlockSpec(memory_space=pl.ANY)
    snap = x * 8 + y * 2 + core
    inverses = [
        lax.dynamic_index_in_dim(
            merge_inverse, 32 // 2 ** (level + 1) - 1 + snap // 2 ** (level + 1), 0, keepdims=False
        )
        for level in range(5)
    ]

    cand, minus, plus, hm, hp, own, keep, send = call(
        pass_kernel,
        (
            shape((RANK, RANK), F32),
            shape((RANK, 2 * width), F32),
            shape((RANK, 2 * width), F32),
            shape((RANK // 2, width), F32),
            shape((RANK // 2, width), F32),
            shape((3, RANK, width), F32),
            shape((half, RANK), BF16),
            shape((half, RANK), BF16),
        ),
        "sketch_pass",
        in_specs=[whole, vmem, vmem, vmem],
        scratch_shapes=[
            pltpu.VMEM((rows, cols), BF16),
            pltpu.VMEM((RANK, cols), F32),
            pltpu.VMEM((cols, 2 * RANK), BF16),
            pltpu.SemaphoreType.DMA((rows // ROW_BLOCK,)),
        ],
    )(snapshots, test_matrix, leaf_pivots, skeleton_ids.reshape(1, RANK))

    got = lax.ppermute(send, "snap", core_swap())
    others = [lax.ppermute(cand, "grid", grid_shift(d)) for d in (4, 3, 5, 2, 6, 1, 7)]
    rm = lax.ppermute(minus, "grid", grid_shift(-1))
    rp = lax.ppermute(plus, "grid", grid_shift(1))
    rhm = lax.ppermute(hm, "grid", grid_shift(-2))
    rhp = lax.ppermute(hp, "grid", grid_shift(2))

    pair = shape((2 * RANK, RANK), BF16)
    message = shape((4 * RANK, RANK), BF16)
    square2 = shape((RANK, 2 * RANK), F32)
    stack = pltpu.VMEM((SIDE, 2 * RANK, RANK), BF16)
    leaf = call(cand_sum_kernel, pair, "cand_sum")(cand, *others)
    leaf_other = lax.ppermute(leaf, "snap", core_swap())
    cand1, mine, *msgs = call(level0_kernel, (pair, pair, message, message, message), "level0")(
        leaf, leaf_other, merge_pivots, keep, got
    )
    got_y = [lax.ppermute(msg, "snap", y_shift(d)) for d, msg in enumerate(msgs, 1)]
    path = call(path0_kernel, square2, "path0")(
        leaf, cand1, merge_pivots, leaf_inverse[0], inverses[0]
    )
    cand2, msg_x = call(level12_kernel, (pair, message), "level12", scratch_shapes=[stack])(
        cand1, mine, *got_y, merge_pivots
    )
    got_x = [lax.ppermute(msg_x, "snap", x_shift(d)) for d in (1, 2, 3)]
    path = call(path12_kernel, square2, "path12")(
        cand1, cand2, msg_x, merge_pivots, inverses[1], inverses[2], path
    )
    path, skel = call(level34_kernel, (square2, pair), "level34", scratch_shapes=[stack])(
        msg_x, *got_x, merge_pivots, inverses[3], inverses[4], path
    )
    down, up = call(
        relay_kernel, (shape((RANK, width), F32), shape((RANK, width), F32)), "relay"
    )(own, rm, rp, rhm, rhp)
    rd = lax.ppermute(down, "grid", grid_shift(-2))
    ru = lax.ppermute(up, "grid", grid_shift(2))
    mapped = call(final_kernel, shape((RANK, width), BF16), "final")(
        path, own, rm, rp, rd, ru, leaf_pivots
    )
    parts = [lax.ppermute(mapped, "grid", grid_shift(d)) for d in range(1, GRID)]
    coefficients = call(place_grid_kernel, shape((RANK, cols), BF16), "place_grid")(mapped, *parts)
    skel_y = [lax.ppermute(skel, "snap", y_shift(d)) for d in (1, 2, 3)]
    skel_half = call(place_y_kernel, shape((half, RANK), BF16), "place_y")(skel, *skel_y)
    skel_other = lax.ppermute(skel_half, "snap", core_swap())
    skeleton = call(place_core_kernel, shape((rows, RANK), BF16), "place_core")(
        skel_half, skel_other
    )
    return (skeleton, coefficients)


def solution(mesh):
    return jax.shard_map(
        per_device,
        mesh=mesh,
        in_specs=(
            P("grid", "snap"),
            P(None, "grid"),
            P("snap", None),
            P("snap", None, None),
            P(),
            P(),
            P(),
        ),
        out_specs=(P("grid", None), P(None, "snap")),
        check_vma=False,
    )
```

```python
import jax
import jax.numpy as jnp
from jax import lax
from jax.experimental import pallas as pl
from jax.experimental.pallas import tpu as pltpu
from jax.sharding import PartitionSpec as P

PRECISE = lax.Precision.HIGHEST
F32 = jnp.float32
BF16 = jnp.bfloat16


GRID = 8
SIDE = 4
CORES = 2
RANK = 128
ROW_BLOCK = 256
FIRST_STEPS = (4, 2, -2)
SECOND_STEPS = (3, -3, 1, -1)


def grid_shift(step):
    return [(i, (i + step) % GRID) for i in range(GRID)]


def split_shift(i):
    pairs = []
    for core, steps in enumerate((FIRST_STEPS, SECOND_STEPS)):
        if i < len(steps):
            for g in range(GRID):
                for s in range(core, SIDE * SIDE * CORES, CORES):
                    to = (g + steps[i]) % GRID
                    pairs.append((g * SIDE * SIDE * CORES + s, to * SIDE * SIDE * CORES + s))
    return pairs


def core_swap():
    return [(i, i ^ 1) for i in range(SIDE * SIDE * CORES)]


def y_shift(step):
    return [
        (x * 8 + y * 2 + c, x * 8 + (y + step) % SIDE * 2 + c)
        for x in range(SIDE)
        for y in range(SIDE)
        for c in range(CORES)
    ]


def x_shift(step):
    return [
        (x * 8 + y * 2 + c, (x + step) % SIDE * 8 + y * 2 + c)
        for x in range(SIDE)
        for y in range(SIDE)
        for c in range(CORES)
    ]


def place():
    snap = lax.axis_index("snap")
    return snap // 8, snap // 2 % SIDE, snap % CORES


def dot(a, b):
    return jnp.dot(a, b, precision=PRECISE, preferred_element_type=F32)


def split(value):
    high = value.astype(BF16)
    low = (value - high.astype(F32)).astype(BF16)
    return high, low


def joined(pair):
    return pair[:RANK].astype(F32) + pair[RANK:].astype(F32)


def pickers(pivots):
    rows = lax.broadcasted_iota(jnp.int32, (RANK, RANK), 0)
    return rows == pivots, rows + RANK == pivots


def select(lower, upper, pivots):
    low_pick, high_pick = pickers(pivots)
    kept = jnp.dot(lower, low_pick.astype(BF16), preferred_element_type=F32) + jnp.dot(
        upper, high_pick.astype(BF16), preferred_element_type=F32
    )
    return kept.astype(BF16)


def portion(kept, own, pivots, side, inverse):
    rows = lax.broadcasted_iota(jnp.int32, (RANK, RANK), 0)
    chosen = (rows + side * RANK == pivots).astype(F32).T
    coeffs = dot(inverse, dot(joined(kept).T, joined(own)))
    mask = jnp.sum(chosen, axis=0, keepdims=True)
    return coeffs * (1.0 - mask) + chosen


def pass_kernel(
    snap_ref, test_ref, piv_ref, ids_ref, cand_ref, minus_ref, plus_ref, hm_ref, hp_ref, own_ref,
    keep_ref, send_ref, buf, acc, hot, sems,
):
    rows, cols = snap_ref.shape
    blocks = rows // ROW_BLOCK
    me = lax.axis_index("grid")
    snap = lax.axis_index("snap")
    core = snap % CORES
    copies = []
    for i in range(blocks):
        span = pl.ds(i * ROW_BLOCK, ROW_BLOCK)
        copy = pltpu.make_async_copy(snap_ref.at[span, :], buf.at[span, :], sems.at[i])
        copy.start()
        copies.append(copy)
    column = lax.broadcasted_iota(jnp.int32, (cols, RANK), 0)
    hot[:, :RANK] = (column == ids_ref[...] - snap * cols).astype(F32).astype(BF16)
    hot[:, RANK:] = (column == piv_ref[...]).astype(F32).astype(BF16)
    cand = jnp.zeros((RANK, RANK), F32)
    for i in range(blocks):
        span = pl.ds(i * ROW_BLOCK, ROW_BLOCK)
        copies[i].wait()
        tile = buf[span, :]
        weights = test_ref[:, span]
        update = jnp.dot(weights, tile, preferred_element_type=F32)
        if i:
            acc[...] += update
        else:
            acc[...] = update
        picked = jnp.dot(tile, hot[...], preferred_element_type=F32).astype(BF16)
        cand = cand + jnp.dot(weights, picked[:, RANK:], preferred_element_type=F32)
        half, inner = divmod(i * ROW_BLOCK, rows // CORES)

        @pl.when(core == half)
        def _():
            keep_ref[pl.ds(inner, ROW_BLOCK), :] = picked[:, :RANK]

        @pl.when(core != half)
        def _():
            send_ref[pl.ds(inner, ROW_BLOCK), :] = picked[:, :RANK]

    cand_ref[...] = cand
    width = cols // GRID

    def chunk(step):
        return acc[:, pl.ds(pl.multiple_of((me + GRID + step) % GRID * width, width), width)]

    minus_ref[:, :width] = chunk(-3)
    minus_ref[:, width:] = chunk(-1)
    plus_ref[:, :width] = chunk(3)
    plus_ref[:, width:] = chunk(1)
    far = chunk(4)
    hm_ref[...] = far[: RANK // 2]
    hp_ref[...] = far[RANK // 2 :]
    own_ref[0] = chunk(0)
    own_ref[1] = chunk(-2)
    own_ref[2] = chunk(2)


def shape(dims, dtype):
    return jax.ShapeDtypeStruct(dims, dtype)


def near(value):
    return pltpu.with_memory_space_constraint(value, pltpu.VMEM)


def call(kernel, outs, far=False, **options):
    spec = pl.BlockSpec(memory_space=pltpu.VMEM)
    single = not isinstance(outs, tuple)
    listed = (outs,) if single else outs
    placed = tuple(out if far else pltpu.VMEM(out.shape, out.dtype) for out in listed)
    options.setdefault("out_specs", spec if single else (spec,) * len(listed))
    body = pl.pallas_call(kernel, out_shape=placed[0] if single else placed, **options)

    def run(*args):
        return body(*(near(arg) for arg in args))

    return run


def both_kernel(own_ref, other_ref, out_ref):
    _, _, core = place()
    out_ref[core] = own_ref[...]
    out_ref[1 - core] = other_ref[...]


def half_sum_kernel(both_ref, r1, r2, r3, r4, out_ref):
    _, _, core = place()
    total = (r1[...] + r2[...]) + (r3[...] + r4[...])
    out_ref[...] = total + jnp.where(core == 0, both_ref[...], 0.0)


def level0_kernel(mine_ref, other_ref, mp_ref, leaf_ref, cand_ref):
    x, y, core = place()
    pivots = mp_ref[pl.ds(15 + x * SIDE + y, 1), :]
    parts = []
    for block in range(CORES):
        high, low = split(mine_ref[block] + other_ref[block])
        parts.append(jnp.concatenate([high, low], axis=0))
    leaf_ref[...] = jnp.where(core == 0, parts[0], parts[1])
    cand_ref[...] = select(parts[0], parts[1], pivots)


def spread_y_kernel(keep_ref, got_ref, mine_ref, *msg_refs):
    _, y, _ = place()
    for d, ref in enumerate((mine_ref, *msg_refs)):
        span = pl.ds(pl.multiple_of((y + d) % SIDE * 2 * RANK, 2 * RANK), 2 * RANK)
        ref[...] = keep_ref[span, :] + got_ref[span, :]


def sum_y_kernel(mine_ref, r1, r2, r3, out_ref):
    out_ref[...] = mine_ref[...] + r1[...] + (r2[...] + r3[...])


def path0_kernel(own_ref, cand_ref, mp_ref, li_ref, mi_ref, out_ref):
    x, y, core = place()
    pivots = mp_ref[pl.ds(15 + x * SIDE + y, 1), :]
    leaf = dot(li_ref[...], joined(own_ref[...]).T)
    part = portion(cand_ref[...], own_ref[...], pivots, core, mi_ref[...])
    out_ref[:, :RANK] = dot(part, leaf)
    out_ref[:, RANK:] = part


def two_levels(stack, mp_ref, low_row, high_row):
    first = select(stack[0], stack[1], mp_ref[pl.ds(low_row, 1), :])
    second = select(stack[2], stack[3], mp_ref[pl.ds(low_row + 1, 1), :])
    top = select(first, second, mp_ref[pl.ds(high_row, 1), :])
    return first, second, top


def gather_four(own, msg_refs, at, stack):
    stack[at] = own
    for d, ref in enumerate(msg_refs, 1):
        stack[(at + SIDE - d) % SIDE] = ref[: 2 * RANK]


def level12_kernel(own_ref, mine_ref, r1, r2, r3, mp_ref, cand_ref, msg_ref, stack):
    x, y, _ = place()
    gather_four(own_ref[...], (r1, r2, r3), y, stack)
    first, second, top = two_levels(stack, mp_ref, 7 + x * 2, 3 + x)
    cand_ref[...] = jnp.where(y < 2, first, second)
    msg_ref[: 2 * RANK] = top
    msg_ref[2 * RANK :] = mine_ref[...]


def path12_kernel(own_ref, cand_ref, msg_ref, mp_ref, mi_a_ref, mi_b_ref, path_ref, out_ref):
    x, y, _ = place()
    low = portion(
        cand_ref[...], own_ref[...], mp_ref[pl.ds(7 + x * 2 + y // 2, 1), :], y % 2, mi_a_ref[...]
    )
    high = portion(
        msg_ref[: 2 * RANK], cand_ref[...], mp_ref[pl.ds(3 + x, 1), :], y // 2, mi_b_ref[...]
    )
    out_ref[...] = dot(high, dot(low, path_ref[...]))


def level34_kernel(
    msg_ref, r1, r2, r3, mp_ref, mi_a_ref, mi_b_ref, path_ref, out_ref, skel_ref, stack
):
    x, _, _ = place()
    own = msg_ref[: 2 * RANK]
    skel_ref[...] = msg_ref[2 * RANK :] + r1[2 * RANK :] + (r2[2 * RANK :] + r3[2 * RANK :])
    gather_four(own, (r1, r2, r3), x, stack)
    first, second, top = two_levels(stack, mp_ref, 1, 0)
    mid = jnp.where(x < 2, first, second)
    low = portion(mid, own, mp_ref[pl.ds(1 + x // 2, 1), :], x % 2, mi_a_ref[...])
    high = portion(top, mid, mp_ref[pl.ds(0, 1), :], x // 2, mi_b_ref[...])
    out_ref[...] = dot(high, dot(low, path_ref[...]))


def relay_kernel(own_ref, rm_ref, rp_ref, hm_ref, hp_ref, down_ref, up_ref):
    half = RANK // 2
    width = own_ref.shape[2]
    down = own_ref[1] + rm_ref[:, :width]
    up = own_ref[2] + rp_ref[:, :width]
    down_ref[:half] = down[:half] + hm_ref[...]
    down_ref[half:] = down[half:]
    up_ref[:half] = up[:half]
    up_ref[half:] = up[half:] + hp_ref[...]


def final_kernel(path_ref, own_ref, rm_ref, rp_ref, d_ref, u_ref, piv_ref, out_ref):
    width = own_ref.shape[2]
    me = lax.axis_index("grid")
    z = own_ref[0] + rm_ref[:, width:] + rp_ref[:, width:] + (d_ref[...] + u_ref[...])
    rows = lax.broadcasted_iota(jnp.int32, (width, RANK), 0) + me * width
    chosen = (rows == piv_ref[...]).astype(F32).T
    mask = jnp.sum(chosen, axis=0, keepdims=True)
    stacked = jnp.concatenate([z * (1.0 - mask), chosen], axis=0)
    out_ref[...] = dot(path_ref[...], stacked).astype(BF16)


def both_final_kernel(own_ref, other_ref, out_ref):
    _, _, core = place()
    out_ref[pl.ds(pl.multiple_of(core * RANK, RANK), RANK), :] = own_ref[...]
    out_ref[pl.ds(pl.multiple_of((1 - core) * RANK, RANK), RANK), :] = other_ref[...]


def forward_kernel(r1, r2, r3, r4, out_ref):
    _, _, core = place()
    span = pl.ds(pl.multiple_of((1 - core) * RANK, RANK), RANK)
    for i, ref in enumerate((r1, r2, r3, r4)):
        out_ref[i] = ref[span, :]


def place_grid_kernel(own_ref, r1, r2, r3, r4, other_ref, out_ref, sems):
    _, _, core = place()
    width = own_ref.shape[1]
    me = lax.axis_index("grid")
    span = pl.ds(pl.multiple_of(core * RANK, RANK), RANK)

    def copy(ref, step, i):
        at = pl.multiple_of((me + 2 * GRID - step) % GRID * width, width)
        return pltpu.make_async_copy(ref, out_ref.at[:, pl.ds(at, width)], sems.at[i])

    copies = [copy(own_ref, 0, 0)]
    for i, ref in enumerate((r1, r2, r3)):
        first, second = FIRST_STEPS[i], SECOND_STEPS[i]
        copies.append(copy(ref.at[span, :], first + core * (second - first), 2 * i + 1))
        copies.append(copy(other_ref.at[i], second + core * (first - second), 2 * i + 2))
    for item in copies:
        item.start()
    here = copy(r4.at[span, :], SECOND_STEPS[3], 7)
    there = copy(other_ref.at[3], SECOND_STEPS[3], 7)

    @pl.when(core == 1)
    def _():
        here.start()

    @pl.when(core == 0)
    def _():
        there.start()

    for item in copies:
        item.wait()
    there.wait()


def place_y_kernel(own_ref, r1, r2, r3, out_ref):
    _, y, _ = place()
    height = own_ref.shape[0]
    out_ref[pl.ds(pl.multiple_of(y * height, height), height), :] = own_ref[...]
    for d, ref in enumerate((r1, r2, r3), 1):
        at = (y + SIDE - d) % SIDE
        out_ref[pl.ds(pl.multiple_of(at * height, height), height), :] = ref[...]


def place_core_kernel(own_ref, other_ref, out_ref, sems):
    _, _, core = place()
    height = own_ref.shape[0]
    copies = []
    for i, (ref, at) in enumerate(((own_ref, core), (other_ref, 1 - core))):
        span = pl.ds(pl.multiple_of(at * height, height), height)
        copies.append(pltpu.make_async_copy(ref, out_ref.at[span, :], sems.at[i]))
        copies[-1].start()
    for copy in copies:
        copy.wait()


def per_device(
    snapshots, test_matrix, leaf_pivots, leaf_inverse, merge_pivots, merge_inverse, skeleton_ids
):
    rows, cols = snapshots.shape
    width = cols // GRID
    half = rows // CORES
    x, y, core = place()
    vmem = pl.BlockSpec(memory_space=pltpu.VMEM)
    whole = pl.BlockSpec(memory_space=pl.ANY)
    snap = x * 8 + y * 2 + core
    inverses = [
        lax.dynamic_index_in_dim(
            merge_inverse, 32 // 2 ** (level + 1) - 1 + snap // 2 ** (level + 1), 0, keepdims=False
        )
        for level in range(5)
    ]

    cand, minus, plus, hm, hp, own, keep, send = pl.pallas_call(
        pass_kernel,
        out_shape=(
            pltpu.VMEM((RANK, RANK), F32),
            pltpu.VMEM((RANK, 2 * width), F32),
            pltpu.VMEM((RANK, 2 * width), F32),
            pltpu.VMEM((RANK // 2, width), F32),
            pltpu.VMEM((RANK // 2, width), F32),
            pltpu.VMEM((3, RANK, width), F32),
            pltpu.VMEM((half, RANK), BF16),
            pltpu.VMEM((half, RANK), BF16),
        ),
        name="sketch_pass",
        in_specs=[whole, vmem, vmem, vmem],
        out_specs=(vmem,) * 8,
        scratch_shapes=[
            pltpu.VMEM((rows, cols), BF16),
            pltpu.VMEM((RANK, cols), F32),
            pltpu.VMEM((cols, 2 * RANK), BF16),
            pltpu.SemaphoreType.DMA((rows // ROW_BLOCK,)),
        ],
    )(snapshots, test_matrix, leaf_pivots, skeleton_ids.reshape(1, RANK))

    pair = shape((2 * RANK, RANK), BF16)
    message = shape((4 * RANK, RANK), BF16)
    square2 = shape((RANK, 2 * RANK), F32)
    cubes = shape((CORES, RANK, RANK), F32)
    stack = pltpu.VMEM((SIDE, 2 * RANK, RANK), BF16)

    def swap(value):
        return lax.ppermute(value, "snap", core_swap())

    cand_other = swap(cand)
    got = swap(send)
    both = call(both_kernel, cubes)(cand, cand_other)
    others = [lax.ppermute(both, ("grid", "snap"), split_shift(i)) for i in range(4)]
    mine, *msgs = call(spread_y_kernel, (pair,) * 4)(keep, got)
    skel_y = [lax.ppermute(m, "snap", y_shift(d)) for d, m in enumerate(msgs, 1)]
    mine = call(sum_y_kernel, pair)(mine, *skel_y)
    half_sum = call(half_sum_kernel, cubes)(both, *others)
    half_other = swap(half_sum)
    leaf, cand1 = call(level0_kernel, (pair, pair))(half_sum, half_other, merge_pivots)
    got_y = [lax.ppermute(cand1, "snap", y_shift(d)) for d in (1, 2, 3)]

    rm = lax.ppermute(minus, "grid", grid_shift(-1))
    rp = lax.ppermute(plus, "grid", grid_shift(1))
    rhm = lax.ppermute(hm, "grid", grid_shift(-2))
    rhp = lax.ppermute(hp, "grid", grid_shift(2))

    path = call(path0_kernel, square2)(leaf, cand1, merge_pivots, leaf_inverse[0], inverses[0])
    cand2, msg_x = call(level12_kernel, (pair, message), scratch_shapes=[stack])(
        cand1, mine, *got_y, merge_pivots
    )
    got_x = [lax.ppermute(msg_x, "snap", x_shift(d)) for d in (1, 2, 3)]
    path = call(path12_kernel, square2)(
        cand1, cand2, msg_x, merge_pivots, inverses[1], inverses[2], path
    )
    quarter = shape((RANK, width), F32)
    down, up = call(relay_kernel, (quarter, quarter))(own, rm, rp, rhm, rhp)
    rd = lax.ppermute(down, "grid", grid_shift(-2))
    ru = lax.ppermute(up, "grid", grid_shift(2))
    path, skel = call(level34_kernel, (square2, pair), scratch_shapes=[stack])(
        msg_x, *got_x, merge_pivots, inverses[3], inverses[4], path
    )
    mapped = call(final_kernel, shape((RANK, width), BF16))(path, own, rm, rp, rd, ru, leaf_pivots)

    mapped_other = swap(mapped)
    both_mapped = call(both_final_kernel, shape((2 * RANK, width), BF16))(mapped, mapped_other)
    parts = [lax.ppermute(both_mapped, ("grid", "snap"), split_shift(i)) for i in range(4)]
    skel_y = [lax.ppermute(skel, "snap", y_shift(d)) for d in (1, 2, 3)]
    skel_half = call(place_y_kernel, shape((half, RANK), BF16))(skel, *skel_y)
    skel_other = swap(skel_half)
    forward = call(forward_kernel, shape((4, RANK, width), BF16))(*parts)
    forwarded = swap(forward)
    coefficients = call(
        place_grid_kernel,
        shape((RANK, cols), BF16),
        far=True,
        out_specs=whole,
        scratch_shapes=[pltpu.SemaphoreType.DMA((GRID,))],
    )(mapped, *parts, forwarded)
    skeleton = call(
        place_core_kernel,
        shape((rows, RANK), BF16),
        far=True,
        out_specs=whole,
        scratch_shapes=[pltpu.SemaphoreType.DMA((CORES,))],
    )(skel_half, skel_other)
    return (skeleton, coefficients)


def solution(mesh):
    return jax.shard_map(
        per_device,
        mesh=mesh,
        in_specs=(
            P("grid", "snap"),
            P(None, "grid"),
            P("snap", None),
            P("snap", None, None),
            P(),
            P(),
            P(),
        ),
        out_specs=(P("grid", None), P(None, "snap")),
        check_vma=False,
    )
```

```python
import jax
import jax.numpy as jnp
from jax import lax
from jax.experimental import pallas as pl
from jax.experimental.pallas import tpu as pltpu
from jax.sharding import PartitionSpec as P

PRECISE = lax.Precision.HIGHEST
F32 = jnp.float32
BF16 = jnp.bfloat16


GRID = 8
SIDE = 4
CORES = 2
RANK = 128
ROW_BLOCK = 512
MIB = 2**20
FIRST_STEPS = (4, 2, -2)
SECOND_STEPS = (3, -3, 1, -1)


def grid_shift(step):
    return [(i, (i + step) % GRID) for i in range(GRID)]


def split_shift(i):
    pairs = []
    for core, steps in enumerate((FIRST_STEPS, SECOND_STEPS)):
        if i < len(steps):
            for g in range(GRID):
                for s in range(core, SIDE * SIDE * CORES, CORES):
                    to = (g + steps[i]) % GRID
                    pairs.append((g * SIDE * SIDE * CORES + s, to * SIDE * SIDE * CORES + s))
    return pairs


def way_shift(step):
    pairs = []
    for g in range(GRID):
        for s in range(SIDE * SIDE * CORES):
            to = (g + (2 * (s % CORES) - 1) * step) % GRID
            pairs.append((g * SIDE * SIDE * CORES + s, to * SIDE * SIDE * CORES + s))
    return pairs


def core_swap():
    return [(i, i ^ 1) for i in range(SIDE * SIDE * CORES)]


def y_shift(step):
    return [
        (x * 8 + y * 2 + c, x * 8 + (y + step) % SIDE * 2 + c)
        for x in range(SIDE)
        for y in range(SIDE)
        for c in range(CORES)
    ]


def x_shift(step):
    return [
        (x * 8 + y * 2 + c, (x + step) % SIDE * 8 + y * 2 + c)
        for x in range(SIDE)
        for y in range(SIDE)
        for c in range(CORES)
    ]


def place():
    snap = lax.axis_index("snap")
    return snap // 8, snap // 2 % SIDE, snap % CORES


def dot(a, b):
    return jnp.dot(a, b, precision=PRECISE, preferred_element_type=F32)


def split(value):
    high = value.astype(BF16)
    low = (value - high.astype(F32)).astype(BF16)
    return high, low


def joined(pair):
    return pair[:RANK].astype(F32) + pair[RANK:].astype(F32)


def pickers(pivots):
    rows = lax.broadcasted_iota(jnp.int32, (RANK, RANK), 0)
    return rows == pivots, rows + RANK == pivots


def select(lower, upper, pivots):
    low_pick, high_pick = pickers(pivots)
    kept = jnp.dot(lower, low_pick.astype(BF16), preferred_element_type=F32) + jnp.dot(
        upper, high_pick.astype(BF16), preferred_element_type=F32
    )
    return kept.astype(BF16)


def portion(kept, own, pivots, side, inverse):
    rows = lax.broadcasted_iota(jnp.int32, (RANK, RANK), 0)
    chosen = (rows + side * RANK == pivots).astype(F32).T
    coeffs = dot(inverse, dot(joined(kept).T, joined(own)))
    mask = jnp.sum(chosen, axis=0, keepdims=True)
    return coeffs * (1.0 - mask) + chosen


def pass_kernel(
    snap_ref, test_hbm, piv_hbm, ids_hbm, mi_ref, li_ref,
    cand_ref, own_ref, near_ref, away_ref, keep_ref, send_ref, inv_ref, piv_ref,
    buf, acc, hot, test_ref, ids_ref, sems, inv_sems,
):
    rows, cols = snap_ref.shape
    blocks = rows // ROW_BLOCK
    me = lax.axis_index("grid")
    snap = lax.axis_index("snap")
    core = snap % CORES
    first = [
        pltpu.make_async_copy(piv_hbm, piv_ref, inv_sems.at[6]),
        pltpu.make_async_copy(ids_hbm, ids_ref, inv_sems.at[7]),
        pltpu.make_async_copy(test_hbm, test_ref, inv_sems.at[8]),
    ]
    for copy in first:
        copy.start()
    copies = []
    for i in range(blocks):
        span = pl.ds(i * ROW_BLOCK, ROW_BLOCK)
        copy = pltpu.make_async_copy(snap_ref.at[span, :], buf.at[span, :], sems.at[i])
        copy.start()
        copies.append(copy)
    fetches = [pltpu.make_async_copy(li_ref.at[0], inv_ref.at[0], inv_sems.at[0])]
    for level in range(5):
        node = 32 // 2 ** (level + 1) - 1 + snap // 2 ** (level + 1)
        fetches.append(
            pltpu.make_async_copy(mi_ref.at[node], inv_ref.at[level + 1], inv_sems.at[level + 1])
        )
    for fetch in fetches:
        fetch.start()
    first[0].wait()
    first[1].wait()
    column = lax.broadcasted_iota(jnp.int32, (cols, RANK), 0)
    hot[:, :RANK] = (column == ids_ref[...] - snap * cols).astype(F32).astype(BF16)
    hot[:, RANK:] = (column == piv_ref[...]).astype(F32).astype(BF16)
    first[2].wait()
    cand = jnp.zeros((RANK, RANK), F32)
    for i in range(blocks):
        span = pl.ds(i * ROW_BLOCK, ROW_BLOCK)
        copies[i].wait()
        weights = test_ref[:, span]
        update = jnp.dot(weights, buf[span, :], preferred_element_type=F32)
        if i:
            acc[...] += update
        else:
            acc[...] = update
        picked = []
        for j in range(ROW_BLOCK // RANK):
            part = pl.ds(i * ROW_BLOCK + j * RANK, RANK)
            picked.append(jnp.dot(buf[part, :], hot[...], preferred_element_type=F32).astype(BF16))
        picked = jnp.concatenate(picked, axis=0)
        cand = cand + jnp.dot(weights, picked[:, RANK:], preferred_element_type=F32)
        half, inner = divmod(i * ROW_BLOCK, rows // CORES)

        @pl.when(core == half)
        def _():
            keep_ref[pl.ds(inner, ROW_BLOCK), :] = picked[:, :RANK]

        @pl.when(core != half)
        def _():
            send_ref[pl.ds(inner, ROW_BLOCK), :] = picked[:, :RANK]

    cand_ref[...] = cand
    width = cols // GRID

    def chunk(step):
        return acc[:, pl.ds(pl.multiple_of((me + 2 * GRID + step) % GRID * width, width), width)]

    own_ref[...] = chunk(0)
    far = chunk(4)
    lower, upper = far[: RANK // 2], far[RANK // 2 :]
    for ref, way in ((near_ref, 2 * core - 1), (away_ref, 1 - 2 * core)):
        ref[:, :width] = chunk(3 * way)
        ref[:, width : 2 * width] = chunk(way)
        ref[:, 2 * width : 3 * width] = chunk(2 * way)
        ref[:, 3 * width :] = jnp.concatenate(
            [jnp.where(way < 0, lower, upper)[:, :RANK], jnp.where(way < 0, lower, upper)[:, RANK:]],
            axis=0,
        )
    for fetch in fetches:
        fetch.wait()


def shape(dims, dtype):
    return jax.ShapeDtypeStruct(dims, dtype)


def near(value):
    return pltpu.with_memory_space_constraint(value, pltpu.VMEM)


def call(kernel, outs, far=False, **options):
    spec = pl.BlockSpec(memory_space=pltpu.VMEM)
    single = not isinstance(outs, tuple)
    listed = (outs,) if single else outs
    placed = tuple(out if far else pltpu.VMEM(out.shape, out.dtype) for out in listed)
    options["compiler_params"] = pltpu.CompilerParams(vmem_limit_bytes=4 * MIB)
    options.setdefault("out_specs", spec if single else (spec,) * len(listed))
    body = pl.pallas_call(kernel, out_shape=placed[0] if single else placed, **options)

    def run(*args):
        return body(*(near(arg) for arg in args))

    return run


def both_kernel(own_ref, other_ref, out_ref):
    _, _, core = place()
    out_ref[core] = own_ref[...]
    out_ref[1 - core] = other_ref[...]


def pair_kernel(both_ref, one_ref, out_ref):
    out_ref[...] = both_ref[...] + one_ref[...]


def half_sum_kernel(one_ref, pair_ref, two_ref, far_ref, out_ref):
    _, _, core = place()
    for block in range(CORES):
        near_part = jnp.where(core == 0, pair_ref[block], one_ref[block]) + two_ref[block]
        out_ref[block] = near_part + jnp.where(core == block, far_ref[...], 0.0)


def level0_kernel(
    mine_ref, other_ref, mp_ref, keep_ref, got_ref, leaf_ref, cand_ref, rows_ref, *msg_refs
):
    x, y, core = place()
    pivots = mp_ref[pl.ds(15 + x * SIDE + y, 1), :]
    parts = []
    for block in range(CORES):
        high, low = split(mine_ref[block] + other_ref[block])
        parts.append(jnp.concatenate([high, low], axis=0))
    leaf_ref[...] = jnp.where(core == 0, parts[0], parts[1])
    cand = select(parts[0], parts[1], pivots)
    cand_ref[...] = cand

    def skeleton(d):
        span = pl.ds(pl.multiple_of((y + d) % SIDE * 2 * RANK, 2 * RANK), 2 * RANK)
        return keep_ref[span, :] + got_ref[span, :]

    rows_ref[...] = skeleton(0)
    for d, ref in enumerate(msg_refs, 1):
        ref[: 2 * RANK] = cand
        ref[2 * RANK :] = skeleton(d)


def path0_kernel(own_ref, cand_ref, mp_ref, inv_ref, out_ref):
    x, y, core = place()
    pivots = mp_ref[pl.ds(15 + x * SIDE + y, 1), :]
    leaf = dot(inv_ref[0], joined(own_ref[...]).T)
    part = portion(cand_ref[...], own_ref[...], pivots, core, inv_ref[1])
    out_ref[:, :RANK] = dot(part, leaf)
    out_ref[:, RANK:] = part


def two_levels(stack, mp_ref, low_row, high_row):
    first = select(stack[0], stack[1], mp_ref[pl.ds(low_row, 1), :])
    second = select(stack[2], stack[3], mp_ref[pl.ds(low_row + 1, 1), :])
    top = select(first, second, mp_ref[pl.ds(high_row, 1), :])
    return first, second, top


def gather_four(own, msg_refs, at, stack):
    stack[at] = own
    for d, ref in enumerate(msg_refs, 1):
        stack[(at + SIDE - d) % SIDE] = ref[: 2 * RANK]


def level12_kernel(own_ref, mine_ref, r1, r2, r3, mp_ref, cand_ref, msg_ref, stack):
    x, y, _ = place()
    gather_four(own_ref[...], (r1, r2, r3), y, stack)
    first, second, top = two_levels(stack, mp_ref, 7 + x * 2, 3 + x)
    cand_ref[...] = jnp.where(y < 2, first, second)
    msg_ref[: 2 * RANK] = top
    msg_ref[2 * RANK :] = (
        mine_ref[...] + r1[2 * RANK :] + (r2[2 * RANK :] + r3[2 * RANK :])
    )


def path12_kernel(own_ref, cand_ref, msg_ref, mp_ref, inv_ref, path_ref, out_ref):
    x, y, _ = place()
    low = portion(
        cand_ref[...], own_ref[...], mp_ref[pl.ds(7 + x * 2 + y // 2, 1), :], y % 2, inv_ref[2]
    )
    high = portion(
        msg_ref[: 2 * RANK], cand_ref[...], mp_ref[pl.ds(3 + x, 1), :], y // 2, inv_ref[3]
    )
    out_ref[...] = dot(high, dot(low, path_ref[...]))


def level34_kernel(
    msg_ref, r1, r2, r3, mp_ref, inv_ref, path_ref, out_ref, skel_ref, stack
):
    x, _, _ = place()
    own = msg_ref[: 2 * RANK]
    skel_ref[...] = msg_ref[2 * RANK :] + r1[2 * RANK :] + (r2[2 * RANK :] + r3[2 * RANK :])
    gather_four(own, (r1, r2, r3), x, stack)
    first, second, top = two_levels(stack, mp_ref, 1, 0)
    mid = jnp.where(x < 2, first, second)
    low = portion(mid, own, mp_ref[pl.ds(1 + x // 2, 1), :], x % 2, inv_ref[4])
    high = portion(top, mid, mp_ref[pl.ds(0, 1), :], x // 2, inv_ref[5])
    out_ref[...] = dot(high, dot(low, path_ref[...]))


def pack_kernel(near_ref, got_ref, own_ref, a_ref, h_ref, two_ref, own_out_ref):
    width = two_ref.shape[2]
    for i, ref in enumerate((near_ref, got_ref)):
        a_ref[i] = ref[:, : 2 * width]
        two_ref[i] = ref[:, 2 * width : 3 * width]
        h_ref[i] = ref[:, 3 * width :]
    own_out_ref[...] = own_ref[...]


def relay_kernel(own_ref, two_ref, a_ref, h_ref, out_ref, keep_ref, send_ref):
    _, _, core = place()
    half = RANK // 2
    width = two_ref.shape[2]
    down = core == 0
    for i in range(CORES):
        total = two_ref[i] + a_ref[i, :, :width]
        far = jnp.concatenate([h_ref[i, :half], h_ref[i, half:]], axis=1)
        out_ref[i, :half] = total[:half] + jnp.where(down, far, 0.0)
        out_ref[i, half:] = total[half:] + jnp.where(down, 0.0, far)
    keep_ref[...] = own_ref[...] + a_ref[0, :, width:]
    send_ref[...] = a_ref[1, :, width:]


def ends_kernel(keep_in_ref, send_in_ref, u_ref, piv_ref, keep_ref, send_ref, chosen_ref):
    width = keep_ref.shape[1]
    me = lax.axis_index("grid")
    keep_ref[...] = keep_in_ref[...] + u_ref[0]
    send_ref[...] = send_in_ref[...] + u_ref[1]
    rows = lax.broadcasted_iota(jnp.int32, (width, RANK), 0) + me * width
    chosen_ref[...] = (rows == piv_ref[...]).astype(F32).T


def final_kernel(path_ref, keep_ref, got_ref, chosen_ref, out_ref):
    chosen = chosen_ref[...]
    mask = jnp.sum(chosen, axis=0, keepdims=True)
    z = (keep_ref[...] + got_ref[...]) * (1.0 - mask)
    out_ref[...] = dot(path_ref[...], jnp.concatenate([z, chosen], axis=0)).astype(BF16)


def both_final_kernel(own_ref, other_ref, out_ref):
    _, _, core = place()
    out_ref[pl.ds(pl.multiple_of(core * RANK, RANK), RANK), :] = own_ref[...]
    out_ref[pl.ds(pl.multiple_of((1 - core) * RANK, RANK), RANK), :] = other_ref[...]


def forward_kernel(r1, r2, r3, r4, out_ref):
    _, _, core = place()
    span = pl.ds(pl.multiple_of((1 - core) * RANK, RANK), RANK)
    for i, ref in enumerate((r1, r2, r3, r4)):
        out_ref[i] = ref[span, :]


def place_grid_kernel(own_ref, r1, r2, r3, r4, other_ref, out_ref, sems):
    _, _, core = place()
    width = own_ref.shape[1]
    me = lax.axis_index("grid")
    span = pl.ds(pl.multiple_of(core * RANK, RANK), RANK)

    def copy(ref, step, i):
        at = pl.multiple_of((me + 2 * GRID - step) % GRID * width, width)
        return pltpu.make_async_copy(ref, out_ref.at[:, pl.ds(at, width)], sems.at[i])

    copies = [copy(own_ref, 0, 0)]
    for i, ref in enumerate((r1, r2, r3)):
        first, second = FIRST_STEPS[i], SECOND_STEPS[i]
        copies.append(copy(ref.at[span, :], first + core * (second - first), 2 * i + 1))
        copies.append(copy(other_ref.at[i], second + core * (first - second), 2 * i + 2))
    for item in copies:
        item.start()
    here = copy(r4.at[span, :], SECOND_STEPS[3], 7)
    there = copy(other_ref.at[3], SECOND_STEPS[3], 7)

    @pl.when(core == 1)
    def _():
        here.start()

    @pl.when(core == 0)
    def _():
        there.start()

    for item in copies:
        item.wait()
    there.wait()


def place_y_kernel(own_ref, r1, r2, r3, out_ref):
    _, y, _ = place()
    height = own_ref.shape[0]
    out_ref[pl.ds(pl.multiple_of(y * height, height), height), :] = own_ref[...]
    for d, ref in enumerate((r1, r2, r3), 1):
        at = (y + SIDE - d) % SIDE
        out_ref[pl.ds(pl.multiple_of(at * height, height), height), :] = ref[...]


def place_core_kernel(own_ref, other_ref, out_ref, sems):
    _, _, core = place()
    height = own_ref.shape[0]
    copies = []
    for i, (ref, at) in enumerate(((own_ref, core), (other_ref, 1 - core))):
        span = pl.ds(pl.multiple_of(at * height, height), height)
        copies.append(pltpu.make_async_copy(ref, out_ref.at[span, :], sems.at[i]))
        copies[-1].start()
    for copy in copies:
        copy.wait()


def per_device(
    snapshots, test_matrix, leaf_pivots, leaf_inverse, merge_pivots, merge_inverse, skeleton_ids
):
    rows, cols = snapshots.shape
    width = cols // GRID
    half = rows // CORES
    x, y, core = place()
    vmem = pl.BlockSpec(memory_space=pltpu.VMEM)
    hbm = pl.BlockSpec(memory_space=pltpu.HBM)
    cand, own, near, away, keep, send, inverses, pivots = pl.pallas_call(
        pass_kernel,
        out_shape=(
            pltpu.VMEM((RANK, RANK), F32),
            pltpu.VMEM((RANK, width), F32),
            pltpu.VMEM((RANK, 3 * width + RANK), F32),
            pltpu.VMEM((RANK, 3 * width + RANK), F32),
            pltpu.VMEM((half, RANK), BF16),
            pltpu.VMEM((half, RANK), BF16),
            pltpu.VMEM((6, RANK, RANK), F32),
            pltpu.VMEM((1, RANK), jnp.int32),
        ),
        name="sketch_pass",
        compiler_params=pltpu.CompilerParams(vmem_limit_bytes=24 * MIB),
        in_specs=[hbm] * 6,
        out_specs=(vmem,) * 8,
        scratch_shapes=[
            pltpu.VMEM((rows, cols), BF16),
            pltpu.VMEM((RANK, cols), F32),
            pltpu.VMEM((cols, 2 * RANK), BF16),
            pltpu.VMEM((RANK, rows), BF16),
            pltpu.VMEM((1, RANK), jnp.int32),
            pltpu.SemaphoreType.DMA((rows // ROW_BLOCK,)),
            pltpu.SemaphoreType.DMA((9,)),
        ],
    )(
        *(
            pltpu.with_memory_space_constraint(value, pltpu.HBM)
            for value in (
                snapshots,
                test_matrix,
                leaf_pivots,
                skeleton_ids.reshape(1, RANK),
                merge_inverse,
                leaf_inverse,
            )
        )
    )

    pair = shape((2 * RANK, RANK), BF16)
    message = shape((4 * RANK, RANK), BF16)
    square2 = shape((RANK, 2 * RANK), F32)
    cubes = shape((CORES, RANK, RANK), F32)
    stack = pltpu.VMEM((SIDE, 2 * RANK, RANK), BF16)

    def swap(value):
        return lax.ppermute(value, "snap", core_swap())

    cand_other = swap(cand)
    got = swap(send)
    both = call(both_kernel, cubes)(cand, cand_other)
    both_axes = ("grid", "snap")
    far = lax.ppermute(cand, "grid", grid_shift(4))
    one = lax.ppermute(both, both_axes, way_shift(1))
    duo = call(pair_kernel, cubes)(both, one)
    two = lax.ppermute(duo, both_axes, way_shift(2))
    half_sum = call(half_sum_kernel, cubes)(one, duo, two, far)
    half_other = swap(half_sum)
    leaf, cand1, mine, *msgs = call(level0_kernel, (pair,) * 3 + (message,) * 3)(
        half_sum, half_other, merge_pivots, keep, got
    )
    got_y = [lax.ppermute(m, "snap", y_shift(d)) for d, m in enumerate(msgs, 1)]

    got_near = swap(away)
    quarter = shape((RANK, width), F32)
    a_both, h_both, two_both, own = call(
        pack_kernel,
        (
            shape((CORES, RANK, 2 * width), F32),
            shape((CORES, RANK, RANK), F32),
            shape((CORES, RANK, width), F32),
            quarter,
        ),
    )(near, got_near, own)
    got_a = lax.ppermute(a_both, both_axes, way_shift(1))
    got_h = lax.ppermute(h_both, both_axes, way_shift(2))
    relay, keep_sum, send_sum = call(
        relay_kernel, (shape((CORES, RANK, width), F32), quarter, quarter)
    )(own, two_both, got_a, got_h)
    got_u = lax.ppermute(relay, both_axes, way_shift(2))
    ends, ends_away, chosen = call(ends_kernel, (quarter,) * 3)(keep_sum, send_sum, got_u, pivots)
    ends_got = swap(ends_away)

    path = call(path0_kernel, square2)(leaf, cand1, merge_pivots, inverses)
    cand2, msg_x = call(level12_kernel, (pair, message), scratch_shapes=[stack])(
        cand1, mine, *got_y, merge_pivots
    )
    got_x = [lax.ppermute(msg_x, "snap", x_shift(d)) for d in (1, 2, 3)]
    path = call(path12_kernel, square2)(
        cand1, cand2, msg_x, merge_pivots, inverses, path
    )
    path, skel = call(level34_kernel, (square2, pair), scratch_shapes=[stack])(
        msg_x, *got_x, merge_pivots, inverses, path
    )
    mapped = call(final_kernel, shape((RANK, width), BF16))(
        path, ends, ends_got, chosen
    )

    mapped_other = swap(mapped)
    both_mapped = call(both_final_kernel, shape((2 * RANK, width), BF16))(mapped, mapped_other)
    parts = [lax.ppermute(both_mapped, ("grid", "snap"), split_shift(i)) for i in range(4)]
    skel_y = [lax.ppermute(skel, "snap", y_shift(d)) for d in (1, 2, 3)]
    skel_half = call(place_y_kernel, shape((half, RANK), BF16))(skel, *skel_y)
    skel_other = swap(skel_half)
    forward = call(forward_kernel, shape((4, RANK, width), BF16))(*parts)
    forwarded = swap(forward)
    coefficients = call(
        place_grid_kernel,
        shape((RANK, cols), BF16),
        far=True,
        out_specs=hbm,
        scratch_shapes=[pltpu.SemaphoreType.DMA((GRID,))],
    )(mapped, *parts, forwarded)
    skeleton = call(
        place_core_kernel,
        shape((rows, RANK), BF16),
        far=True,
        out_specs=hbm,
        scratch_shapes=[pltpu.SemaphoreType.DMA((CORES,))],
    )(skel_half, skel_other)
    return (skeleton, coefficients)


def solution(mesh):
    return jax.shard_map(
        per_device,
        mesh=mesh,
        in_specs=(
            P("grid", "snap"),
            P(None, "grid"),
            P("snap", None),
            P("snap", None, None),
            P(),
            P(),
            P(),
        ),
        out_specs=(P("grid", None), P(None, "snap")),
        check_vma=False,
    )
```
